256 devices in a mesh: ctx: 32 (over x, y, core), head: 8 (over z).
Axes of the slice: x: 4, y: 4, z: 8, core: 2. Of those that a mesh axis runs over, the one named last changes fastest.
Arguments:
- channels: bfloat16 [49152, 4096], P(('ctx', 'head')), may hold values from -6 to 6
- input_state_factors: bfloat16 [49152, 128], P(('ctx', 'head')), may hold values from -6 to 6
- c_coeffs: bfloat16 [49152, 128], P(('ctx', 'head')), may hold values from -6 to 6
- step_size_logits: bfloat16 [49152, 64], P(('ctx', 'head'))
- a_log: float32 [64], P('head')
- skip_gain: float32 [64], P('head'), may hold values from 0.5 to 1.5
- mix_gain: float32 [64, 3], P('head'), may hold values from -0.6 to 0.6
- offsets: int32 [384, 3], P('ctx'), may hold values from 1 to 6, as said below
- cotangent: bfloat16 [49152, 4096], P('ctx', 'head'), may hold values from -6 to 6
Outputs:
- mixed: bfloat16 [49152, 4096], P('ctx', 'head')
- grad_channels: bfloat16 [49152, 4096], P(('ctx', 'head'))
- grad_b: float32 [49152, 128], P(('ctx', 'head'))
- grad_c: float32 [49152, 128], P(('ctx', 'head'))
The draws below stay inside these ranges and needn't reach their ends.
Inputs may be any that keep to these rules, and one draw needn't show every extreme that they name: Each block's 3 offsets are distinct; block b's neighbour in slot k is block b - offsets[b, k], and there is none where that index is negative.
All inputs are finite; a program needn't handle non-finite values.
Results may differ from the reference program's by a relative error of at most 0.0052.
Values may be sent and summed in bfloat16 or wider, within the bound.
No kernel may reach another device: no remote copies, remote signals or barrier semaphores. Data moves between devices by JAX's collectives and lax.ppermute only.
A program may use at most 128 MiB of HBM per device.

```python
import math
import jax
import jax.numpy as jnp
from jax import lax

H = 64
P_SIZE = 64
N = 128
Q = 128
K = 3
PATH_ELEMENTS = 49152
SPANS = 12
REACH = 6
BLOCKS = 384
N_CTX = 32


def draw_step_size_logits(key, part):
    root_random_seed, spot_key = jax.random.split(key)
    starting_displacement = jax.random.normal(root_random_seed, (PATH_ELEMENTS, H), jnp.float32)
    nonzero_block_indices = jax.random.randint(spot_key, (2,), 0, PATH_ELEMENTS)
    element_indices = jnp.arange(PATH_ELEMENTS)
    run_extent = jnp.any(element_indices[:, None] == nonzero_block_indices[None, :], axis=1)
    return jnp.where(run_extent[:, None], jnp.float32(0.8 * PATH_ELEMENTS), starting_displacement).astype(jnp.bfloat16)


def draw_a_log(key, part):
    slow_key, middle_key, fast_key, pick_key = jax.random.split(key, 4)
    slow = jnp.log(jax.random.uniform(slow_key, (H,), jnp.float32, 0.2, 0.8) / PATH_ELEMENTS)
    middle_low = jnp.log(jnp.float32(0.8 / PATH_ELEMENTS))
    middle_high = jnp.log(jnp.float32(0.12 / Q))
    middle = jax.random.uniform(middle_key, (H,), jnp.float32, 0.0, 1.0) * (middle_high - middle_low) + middle_low
    fast = jnp.log(jax.random.uniform(fast_key, (H,), jnp.float32, 1.0 / 50.0, 1.0 / 30.0))
    fast_count = H // 4
    middle_count = H // 4
    ranks = jax.random.permutation(pick_key, H)
    return jnp.where(ranks < fast_count, fast, jnp.where(ranks < fast_count + middle_count, middle, slow))


def draw_offsets(key, part):
    score_key, flag_key = jax.random.split(key)
    scores = jax.random.randint(score_key, (BLOCKS, REACH), 0, 1 << 20) * REACH + jnp.arange(REACH)[None, :]
    far_flag = jax.random.randint(flag_key, (BLOCKS,), 0, 2)
    blocks = jnp.arange(BLOCKS)
    far_flag = jnp.where(blocks == 0, 0, jnp.where(blocks == 1, 1, far_flag))
    column = jnp.arange(REACH)[None, :]
    scores = jnp.where((far_flag[:, None] == 1) & (column == REACH - 1), -1, scores)
    scores = jnp.where((far_flag[:, None] == 0) & (column == 0), -1, scores)
    order = jnp.argsort(scores, axis=1, stable=True)
    return (order[:, :K] + 1).astype(jnp.int32)


def block_scale(own_key, extent, cuts, smallest, largest):
    factor_of = 1.0
    for dim, parts in cuts:
        heights = jax.random.uniform(jax.random.fold_in(jax.random.fold_in(own_key, 6), dim), (parts,), jnp.float32, smallest / len(cuts), largest / len(cuts))
        factor_of = factor_of * jnp.repeat(jnp.exp(heights), extent[dim] // parts).reshape((-1,) + (1,) * (len(extent) - 1 - dim))
    return factor_of


def normal_values(own_key, shape, deviation, most, cuts=(), held_as=jnp.bfloat16):
    array = jax.random.normal(own_key, shape, jnp.float32) * deviation
    if len(cuts) > 0:
        array = block_scale(own_key, shape, cuts, -0.22, 0.18) * array
    return jnp.clip(array, min=-most, max=most).astype(held_as)


def setup_inputs(seed: int = 0) -> dict:
    arg_keys = jax.random.split(jax.random.key(seed), 10)
    return {
        "channels": normal_values(arg_keys[0], (PATH_ELEMENTS, H * P_SIZE), 1.0, 6.0, ((0, 256),)),
        "input_state_factors": normal_values(arg_keys[1], (PATH_ELEMENTS, N), 1.0, 6.0, ((0, 256),)),
        "c_coeffs": normal_values(arg_keys[2], (PATH_ELEMENTS, N), 1.0, 6.0, ((0, 256),)),
        "step_size_logits": draw_step_size_logits(jax.random.fold_in(arg_keys[9], 71), 0),
        "a_log": draw_a_log(jax.random.fold_in(arg_keys[9], 71), 0),
        "skip_gain": jnp.clip(1.0 + 0.1 * jax.random.normal(arg_keys[5], (H,), jnp.float32), 0.5, 1.5),
        "mix_gain": jnp.clip(jax.random.uniform(arg_keys[6], (H, K), jnp.float32, -0.6, 0.6) * block_scale(arg_keys[6], (H, K), ((0, 8),), -0.4, 0.0), -0.6, 0.6),
        "offsets": draw_offsets(jax.random.fold_in(arg_keys[9], 71), 0),
        "cotangent": normal_values(arg_keys[8], (PATH_ELEMENTS, H * P_SIZE), 1.0, 6.0, ((0, 32), (1, 8))),
    }


PRECISE = lax.Precision.HIGHEST

def straight_cast(value):
    narrow = lax.optimization_barrier(value.astype(jnp.bfloat16))
    return value + lax.stop_gradient(narrow.astype(jnp.float32) - value)

def mix_blocks(own_rows, before, offset_rows, mixing):
    neighbour_count = before.shape[0]
    blocks_in = own_rows.shape[0]
    head_count = mixing.shape[0]
    row_width = own_rows.shape[-1]
    extended = jnp.concatenate([before, own_rows], axis=0)
    result = own_rows.astype(jnp.float32)
    for column in range(offset_rows.shape[1]):
        source = (neighbour_count + jnp.arange(blocks_in, dtype=jnp.int32) - offset_rows[:, column].astype(jnp.int32)).astype(jnp.int32)
        picked = jnp.take(extended, source, axis=0)
        weight = jnp.repeat(mixing[:, column], row_width // head_count)
        result = result + weight * picked.astype(jnp.float32)
    return result

def spread_terms(grad_rows, offset_rows, neighbour_count, mixing):
    blocks_in = grad_rows.shape[0]
    head_count = mixing.shape[0]
    row_width = grad_rows.shape[-1]
    places = jnp.arange(neighbour_count + blocks_in, dtype=jnp.int32)
    result = jnp.zeros((neighbour_count + blocks_in,) + grad_rows.shape[1:], jnp.float32)
    wide_rows = grad_rows.astype(jnp.float32)
    for column in range(offset_rows.shape[1]):
        target = (neighbour_count + jnp.arange(blocks_in, dtype=jnp.int32) - offset_rows[:, column].astype(jnp.int32)).astype(jnp.int32)
        select = (target[:, None] == places[None, :]).astype(jnp.float32)
        weight = jnp.repeat(mixing[:, column], row_width // head_count)
        result = result + jnp.einsum('be,bqf->eqf', select, weight * wide_rows, precision=PRECISE)
    return result

def span_fn(state, chan, b_part, c_part, log_part, skip_gain, in_scale):
    length = log_part.shape[0]
    cum_log = jnp.cumsum(log_part, axis=0)
    scores = jnp.dot(c_part, b_part.T, precision=PRECISE) * in_scale
    causal = jnp.arange(length)[:, None] >= jnp.arange(length)[None, :]
    head_cum = cum_log.T
    log_gap = head_cum[:, :, None] - head_cum[:, None, :]
    decays = jnp.exp(jnp.where(causal[None], log_gap, -1e+30))
    weights = straight_cast(scores[None] * decays)
    y_intra = jnp.einsum('hts,shp->thp', weights, chan, precision=PRECISE)
    end_decay = jnp.exp(cum_log[-1][None, :] - cum_log)
    b_weighted = straight_cast((b_part * in_scale)[:, None, :] * end_decay[:, :, None])
    pieces = jnp.einsum('shn,shp->hpn', b_weighted, chan, precision=PRECISE)
    c_weighted = c_part[:, None, :] * jnp.exp(cum_log)[:, :, None]
    y_state = jnp.einsum('thn,hpn->thp', c_weighted, state, precision=PRECISE)
    outputs = y_intra + y_state + skip_gain[None, :, None] * chan
    return (jnp.exp(cum_log[-1])[:, None, None] * state + pieces, outputs)

def reference(channels, input_state_factors, c_coeffs, step_size_logits, a_log, skip_gain, mix_gain, offsets, cotangent):
    in_scale = 1.0 / math.sqrt(N * PATH_ELEMENTS)
    log_decay = -jnp.exp(a_log)[None, :] * jax.nn.softplus(step_size_logits.astype(jnp.float32))
    chan_g = channels.reshape(N_CTX, SPANS, Q, H, P_SIZE)
    b_g = input_state_factors.reshape(N_CTX, SPANS, Q, N)
    c_g = c_coeffs.reshape(N_CTX, SPANS, Q, N)
    log_g = log_decay.reshape(N_CTX, SPANS, Q, H)

    def run_span(state, element):
        chan, b_part, c_part, log_part = element
        new_state, outputs = span_fn(state, chan.astype(jnp.float32), b_part.astype(jnp.float32), c_part.astype(jnp.float32), log_part, skip_gain, in_scale)
        return (new_state, outputs.astype(jnp.bfloat16).reshape(Q, H * P_SIZE))

    def run_group(state, element):
        ending, rows_out = lax.scan(run_span, state, element)
        return (ending, (rows_out, state))
    zero_state = jnp.zeros((H, P_SIZE, N), jnp.float32)
    _, (out_rows, starts) = lax.scan(run_group, zero_state, (chan_g, b_g, c_g, log_g))
    before = jnp.concatenate([jnp.zeros_like(out_rows[:1, SPANS - REACH:]), out_rows[:-1, SPANS - REACH:]], axis=0)
    offset_g = offsets.reshape(N_CTX, SPANS, K)
    mixed = lax.map(lambda element: mix_blocks(element[0], element[1], element[2], mix_gain).astype(jnp.bfloat16), (out_rows, before, offset_g))
    mixed = mixed.reshape(PATH_ELEMENTS, H * P_SIZE)
    grad_g = cotangent.reshape(N_CTX, SPANS, Q, H * P_SIZE)
    later_grad = jnp.concatenate([grad_g[1:, :REACH], jnp.zeros_like(grad_g[:1, :REACH])], axis=0)
    later_offset = jnp.concatenate([offset_g[1:, :REACH], jnp.zeros_like(offset_g[:1, :REACH])], axis=0)

    def back_mix(element):
        own_grad, own_offset, next_grad, next_offset = element
        own_sums = spread_terms(own_grad, own_offset, REACH, mix_gain)
        later_sums = spread_terms(next_grad, next_offset, REACH, mix_gain)[:REACH]
        padded = jnp.concatenate([jnp.zeros((SPANS - REACH,) + later_sums.shape[1:], jnp.float32), later_sums], axis=0)
        return (own_grad.astype(jnp.float32) + own_sums[REACH:] + padded).astype(jnp.bfloat16)
    grad_out = lax.map(back_mix, (grad_g, offset_g, later_grad, later_offset))
    grad_spans = grad_out.reshape(N_CTX, SPANS, Q, H, P_SIZE)

    def back_group(grad_end, element):
        chan_c, b_c, c_c, log_c, start_state, grad_part_g = element

        def replay(state, piece_in):
            chan, b_part, c_part, log_part = piece_in
            new_state, _ = span_fn(state, chan.astype(jnp.float32), b_part.astype(jnp.float32), c_part.astype(jnp.float32), log_part, skip_gain, in_scale)
            return (new_state, state)
        _, states = lax.scan(replay, start_state, (chan_c, b_c, c_c, log_c))

        def backward_offset(grad_after, piece_in):
            chan, b_part, c_part, log_part, state, grad_part = piece_in

            def span_local(chan_f, b_f, c_f, state_f):
                return span_fn(state_f, chan_f, b_f, c_f, log_part, skip_gain, in_scale)
            _, pull = jax.vjp(span_local, chan.astype(jnp.float32), b_part.astype(jnp.float32), c_part.astype(jnp.float32), state)
            feature_derivative, b_grad, c_grad, state_grad = pull((grad_after, grad_part.astype(jnp.float32)))
            return (state_grad, (feature_derivative.astype(jnp.bfloat16).reshape(Q, H * P_SIZE), b_grad, c_grad))
        grad_start, results = lax.scan(backward_offset, grad_end, (chan_c, b_c, c_c, log_c, states, grad_part_g), reverse=True)
        return (grad_start, results)
    _, (grad_x, grad_b, grad_c) = lax.scan(back_group, zero_state, (chan_g, b_g, c_g, log_g, starts, grad_spans), reverse=True)
    return (mixed, grad_x.reshape(PATH_ELEMENTS, H * P_SIZE), grad_b.reshape(PATH_ELEMENTS, N), grad_c.reshape(PATH_ELEMENTS, N))
```

```python
import functools
import math

import jax
import jax.numpy as jnp
from jax import lax
from jax.experimental import pallas as pl
from jax.experimental.pallas import tpu as pltpu
from jax.sharding import PartitionSpec as P


P_SIZE = 64
N = 128
Q = 128
PRECISE = lax.Precision.HIGHEST
F32 = jnp.float32
BF16 = jnp.bfloat16


def cost(us, moved=0):
    return pl.CostEstimate(flops=int(us * 5.0e8), bytes_accessed=int(moved), transcendentals=0)


def params(**kw):
    return pltpu.CompilerParams(dimension_semantics=("arbitrary",), **kw)


def nn(a, b):
    return lax.dot_general(a, b, (((1,), (0,)), ((), ())), preferred_element_type=F32)


def nt(a, b):
    return lax.dot_general(a, b, (((1,), (1,)), ((), ())), preferred_element_type=F32)


def tn(a, b):
    return lax.dot_general(a, b, (((0,), (0,)), ((), ())), preferred_element_type=F32)


def causal_mask():
    row = lax.broadcasted_iota(jnp.int32, (Q, Q), 0)
    col = lax.broadcasted_iota(jnp.int32, (Q, Q), 1)
    return row >= col


def left_half():
    return lax.broadcasted_iota(jnp.int32, (Q, 2 * P_SIZE), 1) < P_SIZE


def cumulative(ld):
    lower = jnp.where(causal_mask(), 1.0, 0.0).astype(F32)
    dims = (((1,), (1,)), ((), ()))
    rows = lax.dot_general(ld, lower, dims, precision=PRECISE, preferred_element_type=F32)
    cols = lax.dot_general(lower, ld, dims, precision=PRECISE, preferred_element_type=F32)
    return rows, cols


def lane_fill(cols, lane):
    return jnp.broadcast_to(cols[:, lane : lane + 1], (Q, 2 * P_SIZE))


def spread_heads(cols, heads):
    mask = left_half()
    return jnp.concatenate(
        [
            jnp.where(mask, lane_fill(cols, 2 * pair), lane_fill(cols, 2 * pair + 1))
            for pair in range(heads // 2)
        ],
        axis=1,
    )


def pack_kernel(b_ref, c_ref, dt_ref, out_ref):
    tokens = b_ref.shape[0]
    for j in range(out_ref.shape[0]):
        out_ref[j, :tokens, :N] = b_ref[...]
        out_ref[j, :tokens, N:] = c_ref[...]
        out_ref[j, tokens:, :] = dt_ref[j]


def split_kernel(me_ref, in_ref, *out_refs):
    count = len(out_refs)
    width = out_refs[0].shape[1]
    for d, out_ref in enumerate(out_refs):
        target = lax.rem(me_ref[0] + d, count)
        out_ref[...] = in_ref[:, pl.ds(pl.multiple_of(target * width, width), width)]


def gather_copies(sources, places, ext, sems):
    copies = []
    place = 0
    for number, (ref, (start, length)) in enumerate(zip(sources, places)):
        copies.append(
            pltpu.make_async_copy(
                ref.at[pl.ds(start, length)], ext.at[pl.ds(place, length)], sems.at[number]
            )
        )
        place += length
    for copy in copies:
        copy.start()
    for copy in copies:
        copy.wait()


def mix_back_kernel(places, coef_ref, *refs):
    out_ref, ext, sems = refs[-3], refs[-2], refs[-1]
    i = pl.program_id(0)
    steps = out_ref.shape[0]

    @pl.when(i == 0)
    def _():
        gather_copies(refs[:-3], places, ext, sems)

    for u in range(steps):
        acc = ext[steps * i + u].astype(F32)
        for d in range(1, 7):
            acc = acc + coef_ref[u, d - 1 : d, :] * ext[steps * i + u + d].astype(F32)
        out_ref[u] = acc.astype(BF16)


def mix_fore_kernel(places, first, offset_ref, gain_ref, *refs):
    out_ref, ext, sems = refs[-3], refs[-2], refs[-1]
    i = pl.program_id(0)
    steps = out_ref.shape[0]

    @pl.when(i == 0)
    def _():
        gather_copies(refs[: len(places)], places, ext, sems)

    for u in range(steps):
        block = steps * i + u
        acc = ext[6 + block].astype(F32)
        for k in range(offset_ref.shape[1]):
            picked = ext[6 + block - offset_ref[first + block, k]]
            acc = acc + gain_ref[k : k + 1, :] * picked.astype(F32)
        out_ref[u] = acc.astype(BF16)


def mix(kernel, heads, specs, sources, places, steps, first, count, total, into=None):
    width = sources[0].shape[-1]
    args = list(heads) + list(sources) + ([] if into is None else [into])
    return pl.pallas_call(
        kernel,
        grid=(count // steps,),
        in_specs=list(specs) + [pl.BlockSpec(memory_space=pl.ANY)] * (len(args) - len(heads)),
        out_specs=pl.BlockSpec((steps, Q, width), lambda i: (i + first // steps, 0, 0)),
        out_shape=jax.ShapeDtypeStruct((total, Q, width), BF16),
        scratch_shapes=[
            pltpu.VMEM((sum(length for _, length in places), Q, width), BF16),
            pltpu.SemaphoreType.DMA((len(places),)),
        ],
        input_output_aliases={} if into is None else {len(args) - 1: 0},
        compiler_params=params(),
        cost_estimate=cost(0.5 * count),
    )(*args)


def put_pieces(out_ref, state, decay=None):
    pieces = out_ref.shape[0]
    rows = state.shape[0] // pieces
    width = state.shape[1]
    for k in range(pieces):
        out_ref[k, :, :width] = state[k * rows : (k + 1) * rows]
        if decay is not None:
            out_ref[k, :, width:] = decay


def fold_row(row, rows):
    part = row.shape[1] // rows
    return jnp.concatenate([row[:, r * part : (r + 1) * part] for r in range(rows)], axis=0)


def unfold_row(block):
    return jnp.concatenate([block[r : r + 1] for r in range(block.shape[0])], axis=1)


def take_pieces(ref):
    return jnp.concatenate([ref[k] for k in range(ref.shape[0])], axis=0)


def token_rows(ref):
    used = 3 * Q // 2
    return jnp.concatenate([ref[0, :used], ref[1, :used]], axis=0)


def back_state_kernel(ld_ref, g_ref, c_ref, full_ref, cum_ref, row_ref, out_ref, state, total):
    heads = ld_ref.shape[0]
    i = pl.program_id(0)

    @pl.when(i == 0)
    def _():
        state[...] = jnp.zeros_like(state)
        total[...] = jnp.zeros_like(total)

    all_c = token_rows(c_ref)
    fulls = []
    lasts = []
    for u in range(g_ref.shape[0]):
        part = slice(u * Q, (u + 1) * Q)
        rows, cols = cumulative(ld_ref[:, part])
        row_ref[:, part] = rows
        cum = spread_heads(cols, heads)
        cum_ref[u] = cum
        scaled = (g_ref[u].astype(F32) * jnp.exp(cum)).astype(BF16)
        full = tn(all_c[part], scaled)
        full_ref[u] = full
        fulls.append(full)
        lasts.append(cum[Q - 1 : Q, :])
    now = state[...]
    for full, last in zip(fulls[::-1], lasts[::-1]):
        now = jnp.exp(last) * now + full
    state[...] = now
    total[...] = total[...] + sum(lasts)

    @pl.when(i == pl.num_programs(0) - 1)
    def _():
        put_pieces(out_ref, state[...], fold_row(jnp.exp(total[...]), out_ref.shape[1]))


def fore_state_kernel(in_scale, me_ref, cum_ref, b_ref, *refs):
    piece_ref, x_ref, out_ref, x_all, state, sems = refs[-6:]
    parts = refs[:-6]
    count = len(parts)
    i = pl.program_id(0)

    @pl.when(i == 0)
    def _():
        copies = []
        for d, part in enumerate(parts):
            source = lax.rem(me_ref[0] + count - d, count)
            copies.append(pltpu.make_async_copy(part, x_all.at[source], sems.at[d]))
        for copy in copies:
            copy.start()
        state[...] = jnp.zeros_like(state)
        for copy in copies:
            copy.wait()

    all_b = token_rows(b_ref)
    all_x = jnp.concatenate([x_all[2 * i], x_all[2 * i + 1]], axis=0)
    pieces = []
    lasts = []
    for u in range(x_ref.shape[0]):
        part = slice(u * Q, (u + 1) * Q)
        last = cum_ref[u, Q - 1 : Q, :]
        x = all_x[part]
        x_ref[u] = x
        scaled = (x.astype(F32) * jnp.exp(last - cum_ref[u])).astype(BF16)
        piece = tn(all_b[part], scaled) * in_scale
        piece_ref[u] = piece
        pieces.append(piece)
        lasts.append(last)
    now = state[...]
    for piece, last in zip(pieces, lasts):
        now = jnp.exp(last) * now + piece
    state[...] = now

    @pl.when(i == pl.num_programs(0) - 1)
    def _():
        put_pieces(out_ref, now)


def scan_kernel(reverse, decay_ref, in_ref, out_ref):
    count, rows, width = out_ref.shape
    state = jnp.zeros((rows, width), F32)
    for lap in range(count):
        source = count - 1 - lap if reverse else lap
        out_ref[source] = state
        decay = unfold_row(decay_ref[source, :, width:])
        state = decay * state + in_ref[source, :, :width]


def span_kernel(
    in_scale,
    me_ref,
    row_ref,
    cum_ref,
    x_ref,
    g_ref,
    b_ref,
    c_ref,
    full_ref,
    skip_ref,
    end_ref,
    *refs,
):
    y_ref, cg_ref = refs[:2]
    grad_refs = refs[2:-3]
    grads, state, sems = refs[-3:]
    heads = row_ref.shape[0]
    i = pl.program_id(0)
    count = len(grad_refs)
    tokens = grads.shape[1]
    group = pl.num_programs(0) - 1 - i
    slots = [lax.rem(2 * group + k + count - me_ref[0], count) for k in range(2)]

    def put_grad(u, lanes, value):
        start = u * Q
        while start < (u + 1) * Q:
            place = start // tokens
            stop = min((u + 1) * Q, (place + 1) * tokens)
            rows = slice(start - place * tokens, stop - place * tokens)
            grads[slots[place], rows, lanes] = value[start - u * Q : stop - u * Q]
            start = stop

    @pl.when(i == 0)
    def _():
        state[...] = take_pieces(end_ref)

    causal = causal_mask()
    mask = left_half()
    all_b = token_rows(b_ref)
    all_c = token_rows(c_ref)
    for u in range(x_ref.shape[0] - 1, -1, -1):
        part = slice(u * Q, (u + 1) * Q)
        b = all_b[part]
        c = all_c[part]
        scores = nt(c, b) * in_scale
        after = state[...]
        after_low = after.astype(BF16)
        inter = nn(b, after_low) * in_scale
        grad_scores = jnp.zeros((Q, Q), F32)
        x_ends = []
        for pair in range(heads // 2):
            lanes = slice(pair * 2 * P_SIZE, (pair + 1) * 2 * P_SIZE)
            x = x_ref[u, :, lanes]
            g = g_ref[u, :, lanes]
            zero = jnp.zeros_like(x)
            cum = cum_ref[u, :, lanes]
            gap0 = lane_fill(cum, 0) - row_ref[2 * pair : 2 * pair + 1, part]
            gap1 = lane_fill(cum, P_SIZE) - row_ref[2 * pair + 1 : 2 * pair + 2, part]
            decay0 = jnp.exp(jnp.where(causal, gap0, -1e30))
            decay1 = jnp.exp(jnp.where(causal, gap1, -1e30))
            weight0 = (scores * decay0).astype(BF16)
            weight1 = (scores * decay1).astype(BF16)
            x_two = jnp.concatenate([jnp.where(mask, x, zero), jnp.where(mask, zero, x)], axis=0)
            g_two = jnp.concatenate([jnp.where(mask, g, zero), jnp.where(mask, zero, g)], axis=0)
            skip = skip_ref[0:1, lanes]
            xf = x.astype(F32)
            y_ref[u, :, lanes] = (
                nn(jnp.concatenate([weight0, weight1], axis=1), x_two) + skip * xf
            )
            d_weights = nt(g_two, x)
            grad_scores = grad_scores + d_weights[:Q] * decay0 + d_weights[Q:] * decay1
            local = tn(jnp.concatenate([weight0, weight1], axis=0), g_two)
            end_decay = jnp.exp(cum[Q - 1 : Q, :] - cum)
            grad = local + end_decay * inter[:, lanes] + skip * g.astype(F32)
            put_grad(u, lanes, grad.astype(BF16))
            x_ends.append((xf * end_decay).astype(BF16))
        narrow = (grad_scores * in_scale).astype(BF16)
        b_sum = nt(jnp.concatenate(x_ends, axis=1), after_low) * in_scale
        put_grad(u, slice(heads * P_SIZE, None), (b_sum + tn(narrow, c)).astype(BF16))
        cg_ref[u] = nn(narrow, b)
        state[...] = jnp.exp(cum_ref[u, Q - 1 : Q, :]) * after + full_ref[u]

    @pl.when(i == pl.num_programs(0) - 1)
    def _():
        copies = [
            pltpu.make_async_copy(grads.at[d], ref, sems.at[d]) for d, ref in enumerate(grad_refs)
        ]
        for copy in copies:
            copy.start()
        for copy in copies:
            copy.wait()


def output_kernel(
    cum_ref, g_ref, c_ref, y_ref, cg_ref, piece_ref, start_ref, out_ref, c_out_ref, state
):
    @pl.when(pl.program_id(0) == 0)
    def _():
        state[...] = take_pieces(start_ref)

    all_c = token_rows(c_ref)
    now = state[...]
    for u in range(g_ref.shape[0]):
        from_start = jnp.exp(cum_ref[u])
        low = now.astype(BF16)
        out_ref[u] = (y_ref[u] + nn(all_c[u * Q : (u + 1) * Q], low) * from_start).astype(BF16)
        scaled = (g_ref[u].astype(F32) * from_start).astype(BF16)
        c_out_ref[u] = (cg_ref[u] + nt(scaled, low)).astype(BF16)
        now = jnp.exp(cum_ref[u, Q - 1 : Q, :]) * now + piece_ref[u]
    state[...] = now


def join_kernel(me_ref, *refs):
    grad_ref, b_ref = refs[-2:]
    parts = refs[:-2]
    count = len(parts)
    width = grad_ref.shape[1] // count
    total = jnp.zeros(b_ref.shape, F32)
    for d, part in enumerate(parts):
        source = lax.rem(me_ref[0] + count - d, count)
        grad_ref[:, pl.ds(pl.multiple_of(source * width, width), width)] = part[:, :width]
        total = total + part[:, width:].astype(F32)
    b_ref[...] = total


def sum_kernel(in_ref, out_ref):
    total = in_ref[0].astype(F32)
    for j in range(1, in_ref.shape[0]):
        total = total + in_ref[j].astype(F32)
    out_ref[...] = total


def passed_along(value, axis, steps):
    count = lax.axis_size(axis)
    first, last = (max(0, -steps), min(count, count - steps))
    return lax.ppermute(value, axis, [(source, source + steps) for source in range(first, last)])


def body(
    channels,
    input_state_factors,
    c_coeffs,
    step_size_logits,
    a_log,
    skip_gain,
    mix_gain,
    offsets,
    cotangent,
):
    groups = lax.axis_size("head")
    shards = lax.axis_size("ctx")
    tok_dev = channels.shape[0]
    ctx_tok = tok_dev * groups
    spans = ctx_tok // Q
    reach = spans // 2
    heads = a_log.shape[0]
    width = heads * P_SIZE
    in_scale = 1.0 / math.sqrt(N * ctx_tok * shards)

    each = 3
    reach_rows = reach * Q

    def z_swap(value):
        return lax.all_to_all(value, "head", split_axis=0, concat_axis=0, tiled=True)

    def ctx_swap(value):
        return lax.all_to_all(value, "ctx", split_axis=0, concat_axis=0, tiled=True)

    offset_rows = jnp.pad(
        offsets[:reach].astype(BF16), ((0, 16 - reach), (0, width - offsets.shape[1]))
    )
    sent = jnp.concatenate([cotangent[:reach_rows], offset_rows], axis=0)
    later = passed_along(sent, "ctx", -1)

    dt = jnp.pad(
        step_size_logits.T.reshape(groups, heads, tok_dev),
        ((0, 0), (0, 16 - heads), (0, 2 * N - tok_dev)),
    )
    packed = pl.pallas_call(
        pack_kernel,
        grid=(2,),
        in_specs=[
            pl.BlockSpec((tok_dev, N), lambda j: (0, 0)),
            pl.BlockSpec((tok_dev, N), lambda j: (0, 0)),
            pl.BlockSpec((groups // 2, 16, 2 * N), lambda j: (j, 0, 0)),
        ],
        out_specs=pl.BlockSpec((groups // 2, tok_dev + 16, 2 * N), lambda j: (j, 0, 0)),
        out_shape=jax.ShapeDtypeStruct((groups, tok_dev + 16, 2 * N), BF16),
        compiler_params=params(),
        cost_estimate=cost(3.0),
    )(input_state_factors, c_coeffs, dt)
    bcd = z_swap(packed)

    me = lax.axis_index("head").astype(jnp.int32)[None]
    me_spec = pl.BlockSpec(memory_space=pltpu.SMEM)

    def z_shifts(parts):
        moved = [parts[0]]
        for d in range(1, groups):
            pairs = [(source, (source + d) % groups) for source in range(groups)]
            moved.append(lax.ppermute(parts[d], "head", pairs))
        return moved

    chan_parts = pl.pallas_call(
        split_kernel,
        in_specs=[me_spec, pl.BlockSpec(channels.shape, lambda: (0, 0))],
        out_specs=[pl.BlockSpec((tok_dev, width), lambda: (0, 0))] * groups,
        out_shape=[jax.ShapeDtypeStruct((tok_dev, width), BF16)] * groups,
        cost_estimate=cost(3.0),
    )(me, channels)
    x_parts = z_shifts(chan_parts)

    gain = jnp.repeat(mix_gain.T, P_SIZE, axis=1)
    distance = jnp.arange(1, reach + 1, dtype=jnp.int32)
    later_offsets = later[reach_rows : reach_rows + reach, : offsets.shape[1]].astype(jnp.int32)
    all_offsets = jnp.concatenate([offsets, later_offsets], axis=0)
    sources = jnp.stack([all_offsets[d : d + spans] for d in range(1, reach + 1)], axis=1)
    hit = (sources == distance[None, :, None]).astype(F32)
    back_coef = jnp.sum(hit[..., None] * gain[None, None], axis=2)
    back_coef = jnp.pad(back_coef, ((0, 0), (0, 8 - reach), (0, 0)))

    g_rows = mix(
        functools.partial(mix_back_kernel, ((0, spans), (0, reach))),
        (back_coef,),
        [pl.BlockSpec((2, 8, width), lambda i: (i, 0, 0))],
        (cotangent.reshape(spans, Q, width), later[:reach_rows].reshape(reach, Q, width)),
        ((0, spans), (0, reach)),
        2,
        0,
        spans,
        spans,
    )

    dt_rows = jnp.transpose(bcd[:, tok_dev : tok_dev + heads, :tok_dev], (1, 0, 2))
    dt_rows = dt_rows.reshape(heads, ctx_tok)
    log_decay = -jnp.exp(a_log)[:, None] * jax.nn.softplus(dt_rows.astype(F32))

    steps = spans // each

    def coeff_spec(column, order):
        return pl.BlockSpec((2, tok_dev + 16, N), lambda i: (order(i), 0, column))

    def lane_spec(order):
        return pl.BlockSpec((heads, each * Q), lambda i: (0, order(i)))

    def row_spec(columns, order):
        return pl.BlockSpec((each, Q, columns), lambda i: (order(i), 0, 0))

    def whole(shape):
        return pl.BlockSpec(shape, lambda i: (0,) * len(shape))

    def forward(i):
        return i

    def backward(i):
        return steps - 1 - i

    states = [pltpu.VMEM((N, width), F32), pltpu.VMEM((1, width), F32)]
    piece_shape = (shards, N // shards, width + width // (N // shards))
    span_shape = jax.ShapeDtypeStruct((spans, N, width), F32)
    grad_full, cum, cum_rows, back_pieces = pl.pallas_call(
        back_state_kernel,
        grid=(steps,),
        in_specs=[lane_spec(backward), row_spec(width, backward), coeff_spec(1, backward)],
        out_specs=[
            row_spec(width, backward),
            row_spec(width, backward),
            lane_spec(backward),
            whole(piece_shape),
        ],
        out_shape=[
            span_shape,
            span_shape,
            jax.ShapeDtypeStruct((heads, ctx_tok), F32),
            jax.ShapeDtypeStruct(piece_shape, F32),
        ],
        scratch_shapes=states,
        compiler_params=params(),
        cost_estimate=cost(8.0),
    )(log_decay, g_rows, bcd)

    def scan(reverse, decays, got):
        return pl.pallas_call(
            functools.partial(scan_kernel, reverse),
            out_shape=jax.ShapeDtypeStruct((shards, N // shards, width), F32),
            cost_estimate=cost(2.0),
        )(decays, got)

    rev_got = ctx_swap(back_pieces)
    rev_states = scan(True, rev_got, rev_got)
    grad_end = ctx_swap(rev_states)

    own_shape = (shards, N // shards, width)
    any_spec = pl.BlockSpec(memory_space=pl.ANY)
    pieces, x_rows, fore_pieces = pl.pallas_call(
        functools.partial(fore_state_kernel, in_scale),
        grid=(steps,),
        in_specs=[me_spec, row_spec(width, forward), coeff_spec(0, forward)]
        + [any_spec] * groups,
        out_specs=[row_spec(width, forward), row_spec(width, forward), whole(own_shape)],
        out_shape=[
            span_shape,
            jax.ShapeDtypeStruct((spans, Q, width), BF16),
            jax.ShapeDtypeStruct(own_shape, F32),
        ],
        scratch_shapes=[
            pltpu.VMEM((groups, tok_dev, width), BF16),
            states[0],
            pltpu.SemaphoreType.DMA((groups,)),
        ],
        compiler_params=params(),
        cost_estimate=cost(6.0),
    )(me, cum, bcd, *x_parts)
    fwd_got = ctx_swap(fore_pieces)
    fwd_states = scan(False, rev_got, fwd_got)
    state_in = ctx_swap(fwd_states)

    skip = jnp.repeat(skip_gain, P_SIZE)[None, :]
    start_spec = whole((shards, N // shards, width))
    y_part, c_part, *grads = pl.pallas_call(
        functools.partial(span_kernel, in_scale),
        grid=(steps,),
        in_specs=[
            me_spec,
            lane_spec(backward),
            row_spec(width, backward),
            row_spec(width, backward),
            row_spec(width, backward),
            coeff_spec(0, backward),
            coeff_spec(1, backward),
            row_spec(width, backward),
            whole((1, width)),
            start_spec,
        ],
        out_specs=[row_spec(width, backward), row_spec(N, backward)] + [any_spec] * groups,
        out_shape=[
            jax.ShapeDtypeStruct((spans, Q, width), F32),
            jax.ShapeDtypeStruct((spans, Q, N), F32),
        ]
        + [jax.ShapeDtypeStruct((tok_dev, width + N), BF16)] * groups,
        scratch_shapes=[
            pltpu.VMEM((groups, tok_dev, width + N), BF16),
            states[0],
            pltpu.SemaphoreType.DMA((groups,)),
        ],
        compiler_params=params(),
        cost_estimate=cost(20.0),
    )(me, cum_rows, cum, x_rows, g_rows, bcd, bcd, grad_full, skip, grad_end)

    back = z_shifts(grads)

    out_rows, c_rows = pl.pallas_call(
        output_kernel,
        grid=(steps,),
        in_specs=[
            row_spec(width, forward),
            row_spec(width, forward),
            coeff_spec(1, forward),
            row_spec(width, forward),
            row_spec(N, forward),
            row_spec(width, forward),
            start_spec,
        ],
        out_specs=[row_spec(width, forward), row_spec(N, forward)],
        out_shape=[
            jax.ShapeDtypeStruct((spans, Q, width), BF16),
            jax.ShapeDtypeStruct((spans, Q, N), BF16),
        ],
        scratch_shapes=states[:1],
        compiler_params=params(),
        cost_estimate=cost(8.0),
    )(cum, g_rows, bcd, y_part, c_part, pieces, state_in)

    before = passed_along(out_rows[spans - reach :], "ctx", 1)
    c_back = z_swap(c_rows.reshape(groups, tok_dev, N))
    gain_specs = [
        pl.BlockSpec(memory_space=pltpu.SMEM),
        pl.BlockSpec(gain.shape, lambda i: (0, 0)),
    ]
    late = mix(
        functools.partial(mix_fore_kernel, ((0, spans),), reach),
        (offsets, gain),
        gain_specs,
        (out_rows,),
        ((0, spans),),
        2,
        reach,
        spans - reach,
        spans,
    )
    mixed = mix(
        functools.partial(mix_fore_kernel, ((0, reach), (0, reach)), 0),
        (offsets, gain),
        gain_specs,
        (before, out_rows),
        ((0, reach), (0, reach)),
        2,
        0,
        reach,
        spans,
        into=late,
    ).reshape(ctx_tok, width)

    grad_channels, grad_b = pl.pallas_call(
        join_kernel,
        in_specs=[me_spec]
        + [pl.BlockSpec((tok_dev, width + N), lambda: (0, 0))] * groups,
        out_specs=[
            pl.BlockSpec((tok_dev, groups * width), lambda: (0, 0)),
            pl.BlockSpec((tok_dev, N), lambda: (0, 0)),
        ],
        out_shape=[
            jax.ShapeDtypeStruct((tok_dev, groups * width), BF16),
            jax.ShapeDtypeStruct((tok_dev, N), F32),
        ],
        cost_estimate=cost(3.0),
    )(me, *back)
    grad_c = pl.pallas_call(
        sum_kernel,
        out_shape=jax.ShapeDtypeStruct((tok_dev, N), F32),
        cost_estimate=cost(1.0),
    )(c_back)
    return (mixed, grad_channels, grad_b, grad_c)


def solution(mesh):
    placed = (
        P(("ctx", "head"), None),
        P(("ctx", "head"), None),
        P(("ctx", "head"), None),
        P(("ctx", "head"), None),
        P("head"),
        P("head"),
        P("head", None),
        P("ctx", None),
        P("ctx", "head"),
    )
    return jax.shard_map(
        body,
        mesh=mesh,
        in_specs=placed,
        out_specs=(
            P("ctx", "head"),
            P(("ctx", "head"), None),
            P(("ctx", "head"), None),
            P(("ctx", "head"), None),
        ),
        check_vma=False,
    )
```

```python
import functools
import math

import jax
import jax.numpy as jnp
from jax import lax
from jax.experimental import pallas as pl
from jax.experimental.pallas import tpu as pltpu
from jax.sharding import PartitionSpec as P


P_SIZE = 64
N = 128
Q = 128
PRECISE = lax.Precision.HIGHEST
F32 = jnp.float32
BF16 = jnp.bfloat16


def cost(us, moved=0):
    return pl.CostEstimate(flops=int(us * 5.0e8), bytes_accessed=int(moved), transcendentals=0)


def params(grid=True, small=False):
    semantics = ("arbitrary",) if grid else None
    if small:
        return pltpu.CompilerParams(dimension_semantics=semantics, vmem_limit_bytes=12 << 20)
    return pltpu.CompilerParams(dimension_semantics=semantics)


def nn(a, b):
    return lax.dot_general(a, b, (((1,), (0,)), ((), ())), preferred_element_type=F32)


def nt(a, b):
    return lax.dot_general(a, b, (((1,), (1,)), ((), ())), preferred_element_type=F32)


def tn(a, b):
    return lax.dot_general(a, b, (((0,), (0,)), ((), ())), preferred_element_type=F32)


def causal_mask():
    row = lax.broadcasted_iota(jnp.int32, (Q, Q), 0)
    col = lax.broadcasted_iota(jnp.int32, (Q, Q), 1)
    return row >= col


def left_half():
    return lax.broadcasted_iota(jnp.int32, (Q, 2 * P_SIZE), 1) < P_SIZE


def cumulative(ld):
    lower = jnp.where(causal_mask(), 1.0, 0.0).astype(F32)
    dims = (((1,), (1,)), ((), ()))
    rows = lax.dot_general(ld, lower, dims, precision=PRECISE, preferred_element_type=F32)
    cols = lax.dot_general(lower, ld, dims, precision=PRECISE, preferred_element_type=F32)
    return rows, cols


def lane_fill(cols, lane):
    return jnp.broadcast_to(cols[:, lane : lane + 1], (Q, 2 * P_SIZE))


def spread_heads(cols, heads):
    mask = left_half()
    return jnp.concatenate(
        [
            jnp.where(mask, lane_fill(cols, 2 * pair), lane_fill(cols, 2 * pair + 1))
            for pair in range(heads // 2)
        ],
        axis=1,
    )


def pack_kernel(b_ref, c_ref, dt_ref, out_ref):
    tokens = b_ref.shape[0]
    for j in range(out_ref.shape[0]):
        out_ref[j, :tokens, :N] = b_ref[...]
        out_ref[j, :tokens, N:] = c_ref[...]
        out_ref[j, tokens:, :] = dt_ref[j]


def split_kernel(me_ref, in_ref, *out_refs):
    count = len(out_refs)
    width = out_refs[0].shape[1]
    for d, out_ref in enumerate(out_refs):
        target = lax.rem(me_ref[0] + d, count)
        out_ref[...] = in_ref[:, pl.ds(pl.multiple_of(target * width, width), width)]


def gather_copies(sources, places, ext, sems):
    copies = []
    place = 0
    for number, (ref, (start, length)) in enumerate(zip(sources, places)):
        copies.append(
            pltpu.make_async_copy(
                ref.at[pl.ds(start, length)], ext.at[pl.ds(place, length)], sems.at[number]
            )
        )
        place += length
    for copy in copies:
        copy.start()
    for copy in copies:
        copy.wait()


def block_rows(ref, block):
    return ref[pl.ds(pl.multiple_of(block * Q, Q), Q), :]


def mix_back_kernel(places, coef_ref, *refs):
    out_ref, ext, sems = refs[-3], refs[-2], refs[-1]
    i = pl.program_id(0)
    steps = out_ref.shape[0]

    @pl.when(i == 0)
    def _():
        gather_copies(refs[:-3], places, ext, sems)

    for u in range(steps):
        block = steps * i + u
        acc = block_rows(ext, block).astype(F32)
        for d in range(1, 7):
            acc = acc + coef_ref[u, d - 1 : d, :] * block_rows(ext, block + d).astype(F32)
        out_ref[u] = acc.astype(BF16)


def mix_fore_kernel(places, first, offset_ref, gain_ref, *refs):
    out_ref, ext, sems = refs[-3], refs[-2], refs[-1]
    i = pl.program_id(0)
    steps = out_ref.shape[0]

    @pl.when(i == 0)
    def _():
        gather_copies(refs[: len(places)], places, ext, sems)

    for u in range(steps):
        block = steps * i + u
        acc = block_rows(ext, 6 + block).astype(F32)
        for k in range(offset_ref.shape[1]):
            picked = block_rows(ext, 6 + block - offset_ref[first + block, k])
            acc = acc + gain_ref[k : k + 1, :] * picked.astype(F32)
        out_ref[u] = acc.astype(BF16)


def mix(kernel, heads, specs, sources, places, steps, first, count, total, into=None):
    width = sources[0].shape[-1]
    args = list(heads) + list(sources) + ([] if into is None else [into])
    return pl.pallas_call(
        kernel,
        grid=(count // steps,),
        in_specs=list(specs) + [pl.BlockSpec(memory_space=pl.ANY)] * (len(args) - len(heads)),
        out_specs=pl.BlockSpec((steps, Q, width), lambda i: (i + first // steps, 0, 0)),
        out_shape=jax.ShapeDtypeStruct((total, Q, width), BF16),
        scratch_shapes=[
            pltpu.VMEM((sum(length for _, length in places), width), BF16),
            pltpu.SemaphoreType.DMA((len(places),)),
        ],
        input_output_aliases={} if into is None else {len(args) - 1: 0},
        compiler_params=params(True, True),
        cost_estimate=cost(0.5 * count),
    )(*args)


def put_pieces(out_ref, state, decay=None):
    pieces = out_ref.shape[0]
    rows = state.shape[0] // pieces
    width = state.shape[1]
    for k in range(pieces):
        out_ref[k, :, :width] = state[k * rows : (k + 1) * rows]
        if decay is not None:
            out_ref[k, :, width:] = decay


def fold_row(row, rows):
    part = row.shape[1] // rows
    return jnp.concatenate([row[:, r * part : (r + 1) * part] for r in range(rows)], axis=0)


def unfold_row(block):
    return jnp.concatenate([block[r : r + 1] for r in range(block.shape[0])], axis=1)


def take_pieces(ref):
    return jnp.concatenate([ref[k] for k in range(ref.shape[0])], axis=0)


def token_rows(ref):
    used = 3 * Q // 2
    return jnp.concatenate([ref[0, :used], ref[1, :used]], axis=0)


def back_state_kernel(ld_ref, g_ref, c_ref, full_ref, col_ref, row_ref, out_ref, state, total):
    heads = ld_ref.shape[0]
    i = pl.program_id(0)

    @pl.when(i == 0)
    def _():
        state[...] = jnp.zeros_like(state)
        total[...] = jnp.zeros_like(total)

    all_c = token_rows(c_ref)
    fulls = []
    lasts = []
    for u in range(g_ref.shape[0]):
        part = slice(u * Q, (u + 1) * Q)
        rows, cols = cumulative(ld_ref[:, part])
        row_ref[:, part] = rows
        col_ref[u, :, :heads] = cols
        cum = spread_heads(cols, heads)
        scaled = (g_ref[u].astype(F32) * jnp.exp(cum)).astype(BF16)
        full = tn(all_c[part], scaled)
        full_ref[u] = full.astype(BF16)
        fulls.append(full)
        lasts.append(cum[Q - 1 : Q, :])
    now = state[...]
    for full, last in zip(fulls[::-1], lasts[::-1]):
        now = jnp.exp(last) * now + full
    state[...] = now
    total[...] = total[...] + sum(lasts)

    @pl.when(i == pl.num_programs(0) - 1)
    def _():
        put_pieces(out_ref, state[...], fold_row(jnp.exp(total[...]), out_ref.shape[1]))


def fore_state_kernel(in_scale, heads, me_ref, col_ref, b_ref, *refs):
    piece_ref, x_ref, out_ref, x_all, state, sems = refs[-6:]
    parts = refs[:-6]
    count = len(parts)
    i = pl.program_id(0)

    @pl.when(i == 0)
    def _():
        copies = []
        for d, part in enumerate(parts):
            source = lax.rem(me_ref[0] + count - d, count)
            copies.append(pltpu.make_async_copy(part, x_all.at[source], sems.at[d]))
        for copy in copies:
            copy.start()
        state[...] = jnp.zeros_like(state)
        for copy in copies:
            copy.wait()

    all_b = token_rows(b_ref)
    all_x = jnp.concatenate([x_all[2 * i], x_all[2 * i + 1]], axis=0)
    pieces = []
    lasts = []
    for u in range(x_ref.shape[0]):
        part = slice(u * Q, (u + 1) * Q)
        cum = spread_heads(col_ref[u], heads)
        last = cum[Q - 1 : Q, :]
        x = all_x[part]
        x_ref[u] = x
        scaled = (x.astype(F32) * jnp.exp(last - cum)).astype(BF16)
        piece = tn(all_b[part], scaled) * in_scale
        piece_ref[u] = piece.astype(BF16)
        pieces.append(piece)
        lasts.append(last)
    now = state[...]
    for piece, last in zip(pieces, lasts):
        now = jnp.exp(last) * now + piece
    state[...] = now

    @pl.when(i == pl.num_programs(0) - 1)
    def _():
        put_pieces(out_ref, now)


def scan_kernel(reverse, decay_ref, in_ref, out_ref):
    count, rows, width = out_ref.shape
    state = jnp.zeros((rows, width), F32)
    for lap in range(count):
        source = count - 1 - lap if reverse else lap
        out_ref[source] = state
        decay = unfold_row(decay_ref[source, :, width:])
        state = decay * state + in_ref[source, :, :width]


def span_kernel(
    in_scale,
    me_ref,
    row_ref,
    col_ref,
    x_ref,
    g_ref,
    b_ref,
    c_ref,
    full_ref,
    skip_ref,
    end_ref,
    *refs,
):
    y_ref, cg_ref = refs[:2]
    grad_refs = refs[2:-3]
    grads, state, sems = refs[-3:]
    heads = row_ref.shape[0]
    i = pl.program_id(0)
    count = len(grad_refs)
    tokens = grads.shape[1]
    group = pl.num_programs(0) - 1 - i
    slots = [lax.rem(2 * group + k + count - me_ref[0], count) for k in range(2)]

    def put_grad(u, lanes, value):
        start = u * Q
        while start < (u + 1) * Q:
            place = start // tokens
            stop = min((u + 1) * Q, (place + 1) * tokens)
            rows = slice(start - place * tokens, stop - place * tokens)
            grads[slots[place], rows, lanes] = value[start - u * Q : stop - u * Q]
            start = stop

    @pl.when(i == 0)
    def _():
        state[...] = take_pieces(end_ref)

    causal = causal_mask()
    mask = left_half()
    all_b = token_rows(b_ref)
    all_c = token_rows(c_ref)
    for u in range(x_ref.shape[0] - 1, -1, -1):
        part = slice(u * Q, (u + 1) * Q)
        b = all_b[part]
        c = all_c[part]
        scores = nt(c, b) * in_scale
        after = state[...]
        after_low = after.astype(BF16)
        inter = nn(b, after_low) * in_scale
        grad_scores = jnp.zeros((Q, Q), F32)
        cols = col_ref[u]
        x_ends = []
        factors = []
        for pair in range(heads // 2):
            lanes = slice(pair * 2 * P_SIZE, (pair + 1) * 2 * P_SIZE)
            x = x_ref[u, :, lanes]
            g = g_ref[u, :, lanes]
            zero = jnp.zeros_like(x)
            first = lane_fill(cols, 2 * pair)
            second = lane_fill(cols, 2 * pair + 1)
            cum = jnp.where(mask, first, second)
            gap0 = first - row_ref[2 * pair : 2 * pair + 1, part]
            gap1 = second - row_ref[2 * pair + 1 : 2 * pair + 2, part]
            decay0 = jnp.exp(jnp.where(causal, gap0, -1e30))
            decay1 = jnp.exp(jnp.where(causal, gap1, -1e30))
            weight0 = (scores * decay0).astype(BF16)
            weight1 = (scores * decay1).astype(BF16)
            x_two = jnp.concatenate([jnp.where(mask, x, zero), jnp.where(mask, zero, x)], axis=0)
            g_two = jnp.concatenate([jnp.where(mask, g, zero), jnp.where(mask, zero, g)], axis=0)
            skip = skip_ref[0:1, lanes]
            xf = x.astype(F32)
            y = nn(jnp.concatenate([weight0, weight1], axis=1), x_two) + skip * xf
            y_ref[u, :, lanes] = y.astype(BF16)
            d_weights = nt(g_two, x)
            grad_scores = grad_scores + d_weights[:Q] * decay0 + d_weights[Q:] * decay1
            local = tn(jnp.concatenate([weight0, weight1], axis=0), g_two)
            last = cum[Q - 1 : Q, :]
            end_decay = jnp.exp(last - cum)
            factors.append(jnp.exp(last))
            grad = local + end_decay * inter[:, lanes] + skip * g.astype(F32)
            put_grad(u, lanes, grad.astype(BF16))
            x_ends.append((xf * end_decay).astype(BF16))
        narrow = (grad_scores * in_scale).astype(BF16)
        b_sum = nt(jnp.concatenate(x_ends, axis=1), after_low) * in_scale
        put_grad(u, slice(heads * P_SIZE, None), (b_sum + tn(narrow, c)).astype(BF16))
        cg_ref[u] = nn(narrow, b)
        state[...] = jnp.concatenate(factors, axis=1) * after + full_ref[u].astype(F32)

    for d, ref in enumerate(grad_refs):

        @pl.when(jnp.logical_or(slots[0] == d, slots[1] == d))
        def _(d=d, ref=ref):
            pltpu.make_async_copy(grads.at[d], ref, sems.at[d]).start()

    @pl.when(i == pl.num_programs(0) - 1)
    def _():
        for d, ref in enumerate(grad_refs):
            pltpu.make_async_copy(grads.at[d], ref, sems.at[d]).wait()


def output_kernel(
    heads,
    offset_ref,
    gain_ref,
    col_ref,
    g_ref,
    c_ref,
    y_ref,
    cg_ref,
    piece_ref,
    start_ref,
    out_ref,
    tail_ref,
    mixed_ref,
    c_out_ref,
    state,
    kept,
):
    i = pl.program_id(0)
    steps = g_ref.shape[0]

    @pl.when(i == 0)
    def _():
        state[...] = take_pieces(start_ref)

    all_c = token_rows(c_ref)
    now = state[...]
    for u in range(steps):
        cum = spread_heads(col_ref[u], heads)
        from_start = jnp.exp(cum)
        low = now.astype(BF16)
        out = (y_ref[u].astype(F32) + nn(all_c[u * Q : (u + 1) * Q], low) * from_start).astype(BF16)
        out_ref[u] = out
        tail_ref[u] = out
        kept[steps * i + u] = out
        scaled = (g_ref[u].astype(F32) * from_start).astype(BF16)
        c_out_ref[u] = (cg_ref[u] + nt(scaled, low)).astype(BF16)
        now = jnp.exp(cum[Q - 1 : Q, :]) * now + piece_ref[u].astype(F32)
    state[...] = now

    @pl.when(steps * i >= 6)
    def _():
        for u in range(steps):
            block = steps * i + u
            acc = kept[block].astype(F32)
            for k in range(offset_ref.shape[1]):
                picked = kept[block - offset_ref[block, k]]
                acc = acc + gain_ref[k : k + 1, :] * picked.astype(F32)
            mixed_ref[u] = acc.astype(BF16)


def join_kernel(me_ref, *refs):
    grad_ref, b_ref = refs[-2:]
    parts = refs[:-2]
    count = len(parts)
    width = grad_ref.shape[1] // count
    total = jnp.zeros(b_ref.shape, F32)
    for d, part in enumerate(parts):
        source = lax.rem(me_ref[0] + count - d, count)
        grad_ref[:, pl.ds(pl.multiple_of(source * width, width), width)] = part[:, :width]
        total = total + part[:, width:].astype(F32)
    b_ref[...] = total


def sum_kernel(in_ref, out_ref):
    total = in_ref[0].astype(F32)
    for j in range(1, in_ref.shape[0]):
        total = total + in_ref[j].astype(F32)
    out_ref[...] = total


def passed_along(value, axis, steps):
    count = lax.axis_size(axis)
    first, last = (max(0, -steps), min(count, count - steps))
    return lax.ppermute(value, axis, [(source, source + steps) for source in range(first, last)])


def body(
    channels,
    input_state_factors,
    c_coeffs,
    step_size_logits,
    a_log,
    skip_gain,
    mix_gain,
    offsets,
    cotangent,
):
    groups = lax.axis_size("head")
    shards = lax.axis_size("ctx")
    tok_dev = channels.shape[0]
    ctx_tok = tok_dev * groups
    spans = ctx_tok // Q
    reach = spans // 2
    heads = a_log.shape[0]
    width = heads * P_SIZE
    in_scale = 1.0 / math.sqrt(N * ctx_tok * shards)

    each = 3
    reach_rows = reach * Q

    def z_swap(value):
        return lax.all_to_all(value, "head", split_axis=0, concat_axis=0, tiled=True)

    def ctx_swap(value):
        return lax.all_to_all(value, "ctx", split_axis=0, concat_axis=0, tiled=True)

    offset_rows = jnp.pad(
        offsets[:reach].astype(BF16), ((0, 16 - reach), (0, width - offsets.shape[1]))
    )
    sent = jnp.concatenate([cotangent[:reach_rows], offset_rows], axis=0)
    later = passed_along(sent, "ctx", -1)

    dt = jnp.pad(
        step_size_logits.T.reshape(groups, heads, tok_dev),
        ((0, 0), (0, 16 - heads), (0, 2 * N - tok_dev)),
    )
    packed = pl.pallas_call(
        pack_kernel,
        grid=(2,),
        in_specs=[
            pl.BlockSpec((tok_dev, N), lambda j: (0, 0)),
            pl.BlockSpec((tok_dev, N), lambda j: (0, 0)),
            pl.BlockSpec((groups // 2, 16, 2 * N), lambda j: (j, 0, 0)),
        ],
        out_specs=pl.BlockSpec((groups // 2, tok_dev + 16, 2 * N), lambda j: (j, 0, 0)),
        out_shape=jax.ShapeDtypeStruct((groups, tok_dev + 16, 2 * N), BF16),
        compiler_params=params(True, True),
        cost_estimate=cost(3.0),
    )(input_state_factors, c_coeffs, dt)
    bcd = z_swap(packed)

    me = lax.axis_index("head").astype(jnp.int32)[None]
    me_spec = pl.BlockSpec(memory_space=pltpu.SMEM)

    def z_shifts(parts):
        moved = [parts[0]]
        for d in range(1, groups):
            pairs = [(source, (source + d) % groups) for source in range(groups)]
            moved.append(lax.ppermute(parts[d], "head", pairs))
        return moved

    chan_parts = pl.pallas_call(
        split_kernel,
        in_specs=[me_spec, pl.BlockSpec(channels.shape, lambda: (0, 0))],
        out_specs=[pl.BlockSpec((tok_dev, width), lambda: (0, 0))] * groups,
        out_shape=[jax.ShapeDtypeStruct((tok_dev, width), BF16)] * groups,
        compiler_params=params(False),
        cost_estimate=cost(3.0),
    )(me, channels)
    x_parts = z_shifts(chan_parts)

    gain = jnp.repeat(mix_gain.T, P_SIZE, axis=1)
    distance = jnp.arange(1, reach + 1, dtype=jnp.int32)
    later_offsets = later[reach_rows : reach_rows + reach, : offsets.shape[1]].astype(jnp.int32)
    all_offsets = jnp.concatenate([offsets, later_offsets], axis=0)
    sources = jnp.stack([all_offsets[d : d + spans] for d in range(1, reach + 1)], axis=1)
    hit = (sources == distance[None, :, None]).astype(F32)
    back_coef = jnp.sum(hit[..., None] * gain[None, None], axis=2)
    back_coef = jnp.pad(back_coef, ((0, 0), (0, 8 - reach), (0, 0)))

    g_rows = mix(
        functools.partial(mix_back_kernel, ((0, ctx_tok), (0, reach_rows))),
        (back_coef,),
        [pl.BlockSpec((2, 8, width), lambda i: (i, 0, 0))],
        (cotangent, later),
        ((0, ctx_tok), (0, reach_rows)),
        2,
        0,
        spans,
        spans,
    )

    dt_rows = jnp.transpose(bcd[:, tok_dev : tok_dev + heads, :tok_dev], (1, 0, 2))
    dt_rows = dt_rows.reshape(heads, ctx_tok)
    log_decay = -jnp.exp(a_log)[:, None] * jax.nn.softplus(dt_rows.astype(F32))

    steps = spans // each

    def coeff_spec(column, order):
        return pl.BlockSpec((2, tok_dev + 16, N), lambda i: (order(i), 0, column))

    def lane_spec(order):
        return pl.BlockSpec((heads, each * Q), lambda i: (0, order(i)))

    def row_spec(columns, order):
        return pl.BlockSpec((each, Q, columns), lambda i: (order(i), 0, 0))

    def whole(shape):
        return pl.BlockSpec(shape, lambda i: (0,) * len(shape))

    def forward(i):
        return i

    def backward(i):
        return steps - 1 - i

    states = [pltpu.VMEM((N, width), F32), pltpu.VMEM((1, width), F32)]
    piece_shape = (shards, N // shards, width + width // (N // shards))
    span_shape = jax.ShapeDtypeStruct((spans, N, width), BF16)
    grad_full, cum_cols, cum_rows, back_pieces = pl.pallas_call(
        back_state_kernel,
        grid=(steps,),
        in_specs=[lane_spec(backward), row_spec(width, backward), coeff_spec(1, backward)],
        out_specs=[
            row_spec(width, backward),
            row_spec(N, backward),
            lane_spec(backward),
            whole(piece_shape),
        ],
        out_shape=[
            span_shape,
            jax.ShapeDtypeStruct((spans, Q, N), F32),
            jax.ShapeDtypeStruct((heads, ctx_tok), F32),
            jax.ShapeDtypeStruct(piece_shape, F32),
        ],
        scratch_shapes=states,
        compiler_params=params(),
        cost_estimate=cost(8.0),
    )(log_decay, g_rows, bcd)

    def scan(reverse, decays, got):
        return pl.pallas_call(
            functools.partial(scan_kernel, reverse),
            out_shape=jax.ShapeDtypeStruct((shards, N // shards, width), F32),
            compiler_params=params(False, True),
            cost_estimate=cost(2.0),
        )(decays, got)

    rev_got = ctx_swap(back_pieces)
    rev_states = scan(True, rev_got, rev_got)
    grad_end = ctx_swap(rev_states)

    own_shape = (shards, N // shards, width)
    any_spec = pl.BlockSpec(memory_space=pl.ANY)
    pieces, x_rows, fore_pieces = pl.pallas_call(
        functools.partial(fore_state_kernel, in_scale, heads),
        grid=(steps,),
        in_specs=[me_spec, row_spec(N, forward), coeff_spec(0, forward)]
        + [any_spec] * groups,
        out_specs=[row_spec(width, forward), row_spec(width, forward), whole(own_shape)],
        out_shape=[
            span_shape,
            jax.ShapeDtypeStruct((spans, Q, width), BF16),
            jax.ShapeDtypeStruct(own_shape, F32),
        ],
        scratch_shapes=[
            pltpu.VMEM((groups, tok_dev, width), BF16),
            states[0],
            pltpu.SemaphoreType.DMA((groups,)),
        ],
        compiler_params=params(),
        cost_estimate=cost(6.0),
    )(me, cum_cols, bcd, *x_parts)
    fwd_got = ctx_swap(fore_pieces)
    fwd_states = scan(False, rev_got, fwd_got)
    state_in = ctx_swap(fwd_states)

    skip = jnp.repeat(skip_gain, P_SIZE)[None, :]
    start_spec = whole((shards, N // shards, width))
    y_part, c_part, *grads = pl.pallas_call(
        functools.partial(span_kernel, in_scale),
        grid=(steps,),
        in_specs=[
            me_spec,
            lane_spec(backward),
            row_spec(N, backward),
            row_spec(width, backward),
            row_spec(width, backward),
            coeff_spec(0, backward),
            coeff_spec(1, backward),
            row_spec(width, backward),
            whole((1, width)),
            start_spec,
        ],
        out_specs=[row_spec(width, backward), row_spec(N, backward)] + [any_spec] * groups,
        out_shape=[
            jax.ShapeDtypeStruct((spans, Q, width), BF16),
            jax.ShapeDtypeStruct((spans, Q, N), F32),
        ]
        + [jax.ShapeDtypeStruct((tok_dev, width + N), BF16)] * groups,
        scratch_shapes=[
            pltpu.VMEM((groups, tok_dev, width + N), BF16),
            states[0],
            pltpu.SemaphoreType.DMA((groups,)),
        ],
        compiler_params=params(),
        cost_estimate=cost(20.0),
    )(me, cum_rows, cum_cols, x_rows, g_rows, bcd, bcd, grad_full, skip, grad_end)

    back = z_shifts(grads)

    gain_specs = [
        pl.BlockSpec(memory_space=pltpu.SMEM),
        pl.BlockSpec(gain.shape, lambda i: (0, 0)),
    ]
    skipped = steps // 2
    out_rows, out_tail, late, c_rows = pl.pallas_call(
        functools.partial(output_kernel, heads),
        grid=(steps,),
        in_specs=gain_specs
        + [
            row_spec(N, forward),
            row_spec(width, forward),
            coeff_spec(1, forward),
            row_spec(width, forward),
            row_spec(N, forward),
            row_spec(width, forward),
            start_spec,
        ],
        out_specs=[
            row_spec(width, forward),
            row_spec(width, lambda i: jnp.maximum(i - skipped, 0)),
            row_spec(width, lambda i: jnp.maximum(i, skipped)),
            row_spec(N, forward),
        ],
        out_shape=[
            jax.ShapeDtypeStruct((spans, Q, width), BF16),
            jax.ShapeDtypeStruct((reach, Q, width), BF16),
            jax.ShapeDtypeStruct((spans, Q, width), BF16),
            jax.ShapeDtypeStruct((spans, Q, N), BF16),
        ],
        scratch_shapes=[states[0], pltpu.VMEM((spans, Q, width), BF16)],
        compiler_params=params(),
        cost_estimate=cost(8.0),
    )(offsets, gain, cum_cols, g_rows, bcd, y_part, c_part, pieces, state_in)

    before = passed_along(out_tail, "ctx", 1)
    c_back = z_swap(c_rows.reshape(groups, tok_dev, N))
    mixed = mix(
        functools.partial(mix_fore_kernel, ((0, reach_rows), (0, reach_rows)), 0),
        (offsets, gain),
        gain_specs,
        (before.reshape(reach_rows, width), out_rows.reshape(ctx_tok, width)),
        ((0, reach_rows), (0, reach_rows)),
        2,
        0,
        reach,
        spans,
        into=late,
    ).reshape(ctx_tok, width)

    grad_channels, grad_b = pl.pallas_call(
        join_kernel,
        in_specs=[me_spec]
        + [pl.BlockSpec((tok_dev, width + N), lambda: (0, 0))] * groups,
        out_specs=[
            pl.BlockSpec((tok_dev, groups * width), lambda: (0, 0)),
            pl.BlockSpec((tok_dev, N), lambda: (0, 0)),
        ],
        out_shape=[
            jax.ShapeDtypeStruct((tok_dev, groups * width), BF16),
            jax.ShapeDtypeStruct((tok_dev, N), F32),
        ],
        compiler_params=params(False),
        cost_estimate=cost(3.0),
    )(me, *back)
    grad_c = pl.pallas_call(
        sum_kernel,
        out_shape=jax.ShapeDtypeStruct((tok_dev, N), F32),
        compiler_params=params(False, True),
        cost_estimate=cost(1.0),
    )(c_back)
    return (mixed, grad_channels, grad_b, grad_c)


def solution(mesh):
    placed = (
        P(("ctx", "head"), None),
        P(("ctx", "head"), None),
        P(("ctx", "head"), None),
        P(("ctx", "head"), None),
        P("head"),
        P("head"),
        P("head", None),
        P("ctx", None),
        P("ctx", "head"),
    )
    return jax.shard_map(
        body,
        mesh=mesh,
        in_specs=placed,
        out_specs=(
            P("ctx", "head"),
            P(("ctx", "head"), None),
            P(("ctx", "head"), None),
            P(("ctx", "head"), None),
        ),
        check_vma=False,
    )
```
